32 devices in a mesh: samp: 4 (over x, core), pos: 8 (over z, y).
Axes of the slice: x: 2, y: 2, z: 4, core: 2. Of those that a mesh axis runs over, the one named last changes fastest.
Arguments:
- dosages: bfloat16 [16384, 8192], P('samp', 'pos'), may hold values from -64 to 64
- phenotypes: bfloat16 [16384, 3072], P('samp', 'pos'), may hold values from -64 to 64
- window_low: int32 [3072], P('pos'), may hold values from 0 to 8191, as said below
- window_high: int32 [3072], P('pos'), may hold values from 0 to 8191, as said below
Outputs:
- statistics: float32 [8, 2048, 384], P('pos', 'samp')
The draws below stay inside these ranges and needn't reach their ends.
Inputs may be any that keep to these rules, and one draw needn't show every extreme that they name: For peak p in block b = p // 384: b * 1024 - 512 <= window_low[p] <= window_high[p] <= b * 1024 + 1535. In every block but the first, one window starts exactly 512 variants before the block; in every block but the last, one ends exactly 512 variants after it. Same bounds as window_low; window_high[p] >= window_low[p].
All inputs are finite; a program needn't handle non-finite values.
Results may differ from the reference program's by a relative error of at most 0.0003.
Values may be sent and summed in bfloat16 or wider, within the bound.
No kernel may reach another device: no remote copies, remote signals or barrier semaphores. Data moves between devices by JAX's collectives and lax.ppermute only.
A program may use at most 64 MiB of HBM per device.

```python
import math
import jax
import jax.numpy as jnp
from jax import lax

V_DEV = 1024
P_DEV = 384
HALO = 512
SPAN = 2048
BLOCKS = 8
SAMPLES = 16384
VARIANTS = 8192
PEAKS = 3072


def draw_field(key, row_count, col_count):
    key_base, key_cols, key_rows = jax.random.split(key, 3)
    base = jax.random.truncated_normal(key_base, -4.0, 4.0, (row_count, col_count), jnp.float32)
    col_scale = jnp.exp(jax.random.uniform(key_cols, (1, col_count), jnp.float32, jnp.log(0.3), jnp.log(3.0)))
    position = jnp.arange(row_count, dtype=jnp.float32)[:, None] / row_count
    row_mix = 0.5 * position + 0.5 * jax.random.uniform(key_rows, (row_count, 1), jnp.float32)
    row_scale = jnp.exp(jnp.log(0.4) + jnp.log(10.0) * row_mix)
    field = base * row_scale * col_scale
    return field


def draw_dosages(key, part):
    return draw_field(jax.random.fold_in(key, 11), SAMPLES, VARIANTS).astype(jnp.bfloat16)


def draw_phenotypes(key, part):
    return draw_field(jax.random.fold_in(key, 13), SAMPLES, PEAKS).astype(jnp.bfloat16)


def draw_windows(key):
    key_centre, key_left, key_right = jax.random.split(jax.random.fold_in(key, 7), 3)
    peak_index = jnp.arange(PEAKS, dtype=jnp.int32)
    block_index = peak_index // P_DEV
    local_index = peak_index % P_DEV
    block_first = block_index * V_DEV
    centre = block_first + jax.random.randint(key_centre, (PEAKS,), 0, V_DEV, dtype=jnp.int32)
    left_reach = jax.random.randint(key_left, (PEAKS,), HALO // 8, HALO + 1, dtype=jnp.int32)
    right_reach = jax.random.randint(key_right, (PEAKS,), HALO // 8, HALO + 1, dtype=jnp.int32)
    is_first = local_index == 0
    is_last = local_index == P_DEV - 1
    centre = jnp.where(is_first, block_first, jnp.where(is_last, block_first + V_DEV - 1, centre))
    left_reach = jnp.where(is_first, HALO, left_reach)
    right_reach = jnp.where(is_last, HALO, right_reach)
    lows = jnp.maximum(centre - left_reach, 0)
    highs = jnp.minimum(centre + right_reach, VARIANTS - 1)
    return (lows.astype(jnp.int32), highs.astype(jnp.int32))


def draw_window_low(key, part):
    return draw_windows(key)[0]


def draw_window_high(key, part):
    return draw_windows(key)[1]


def setup_inputs(seed: int = 0) -> dict:
    key_of = jax.random.split(jax.random.key(seed), 5)
    dosages = draw_dosages(jax.random.fold_in(key_of[4], 71), 0)
    phenotypes = draw_phenotypes(jax.random.fold_in(key_of[4], 71), 0)
    window_low = draw_window_low(jax.random.fold_in(key_of[4], 71), 0)
    window_high = draw_window_high(jax.random.fold_in(key_of[4], 71), 0)
    return {"dosages": dosages, "phenotypes": phenotypes, "window_low": window_low, "window_high": window_high}


EPS = 1e-06

def sum_squares(values):
    return lax.optimization_barrier(jnp.sum(jnp.square(values.astype(jnp.float32)), axis=0))

def reference(dosages, phenotypes, window_low, window_high):
    padded = jnp.pad(dosages, ((0, 0), (HALO, HALO)))
    factor = math.sqrt(float(SAMPLES - 2))

    def one_block(block_index):
        variant_panel = lax.dynamic_slice_in_dim(padded, (block_index * V_DEV).astype(jnp.int32), SPAN, 1)
        peak_panel = lax.dynamic_slice_in_dim(phenotypes, (block_index * P_DEV).astype(jnp.int32), P_DEV, 1)
        lows = lax.dynamic_slice_in_dim(window_low, (block_index * P_DEV).astype(jnp.int32), P_DEV, 0)
        highs = lax.dynamic_slice_in_dim(window_high, (block_index * P_DEV).astype(jnp.int32), P_DEV, 0)
        cross = lax.dot_general(variant_panel, peak_panel, (((0,), (0,)), ((), ())), preferred_element_type=jnp.float32)
        variant_squares = sum_squares(variant_panel)
        peak_squares = sum_squares(peak_panel)
        variant_index = block_index * V_DEV - HALO + jnp.arange(SPAN, dtype=jnp.int32)[:, None]
        inside = (variant_index >= lows[None, :]) & (variant_index <= highs[None, :])
        scale_terms = (variant_squares[:, None] + EPS) * (peak_squares[None, :] + EPS)
        statistic = factor * cross / jnp.sqrt(scale_terms)
        return jnp.where(inside, statistic, jnp.zeros_like(statistic))
    return lax.map(one_block, jnp.arange(BLOCKS, dtype=jnp.int32))
```

```python
import math

import jax
import jax.numpy as jnp
from jax import lax
from jax.sharding import PartitionSpec as P

HALO = 512
EPS = 1e-06
LANES = 128
ROW_PARTS = 4


def sum_squares(values):
    return jnp.sum(jnp.square(values.astype(jnp.float32)), axis=0)


def cross_rows(variant_panel, phenotypes):
    return lax.dot_general(
        variant_panel, phenotypes, (((0,), (0,)), ((), ())), preferred_element_type=jnp.float32
    )


def chunk_plan(sample_rows, peak_width):
    last = peak_width - LANES if peak_width > LANES and peak_width % LANES == 0 else 0
    plan = [(0, last, [(0, sample_rows)])] if last else []
    step = sample_rows // ROW_PARTS
    plan.append((last, peak_width, [(i * step, (i + 1) * step) for i in range(ROW_PARTS)]))
    return plan


def hop(array, pairs, pos_count):
    return lax.ppermute(array, ("samp", "pos"), [(a * pos_count + b, c * pos_count + d) for a, b, c, d in pairs])


def shards(dosages, phenotypes, window_low, window_high):
    sample_rows, block_width = dosages.shape
    peak_width = phenotypes.shape[1]
    span_width = block_width + 2 * HALO
    samp_count = lax.axis_size("samp")
    pos_count = lax.axis_size("pos")
    samp_index = lax.axis_index("samp")
    pos_index = lax.axis_index("pos")
    share_rows = span_width // samp_count
    halo_shares = HALO // share_rows
    half = samp_count // 2
    even = pos_index % 2 == 0
    all_samp = range(samp_count)
    all_pos = range(pos_count)

    swap = [(b, b ^ 1) for b in all_pos]
    onward = [(b, b + 2) for b in range(0, pos_count - 2, 2)] + [(b, b - 2) for b in range(3, pos_count, 2)]

    plan = chunk_plan(sample_rows, peak_width)
    near, far = [], []
    for low, high, rows in plan:
        near.append([lax.ppermute(phenotypes[a:b, low:high], "pos", swap) for a, b in rows])
    for parts in near:
        far.append([lax.ppermute(part, "pos", onward) for part in parts])

    near_start = jnp.where(even, block_width - HALO, 0)
    far_start = jnp.where(even, 0, block_width - HALO)
    near_panel = lax.dynamic_slice_in_dim(dosages, near_start, HALO, 1)
    far_panel = lax.dynamic_slice_in_dim(dosages, far_start, HALO, 1)

    near_sq, far_sq = sum_squares(near_panel), sum_squares(far_panel)
    squares = jnp.concatenate(
        [jnp.where(even, far_sq, near_sq), jnp.where(even, near_sq, far_sq), sum_squares(phenotypes)]
    )
    bit = 1
    while bit < samp_count:
        squares = squares + lax.ppermute(squares, "samp", [(s, s ^ bit) for s in all_samp])
        bit *= 2
    low_sq, high_sq, peak_total = squares[:HALO], squares[HALO : 2 * HALO], squares[2 * HALO :]
    upward = samp_index < half
    outer_sq = hop(
        jnp.where(upward, high_sq, low_sq),
        [(s, b, s, b + 1) for s in range(half) for b in range(pos_count - 1)]
        + [(s, b, s, b - 1) for s in range(half, samp_count) for b in range(1, pos_count)],
        pos_count,
    )
    outer = (samp_index < halo_shares) | (samp_index >= samp_count - halo_shares)
    variant_total = jnp.where(outer, outer_sq, jnp.where(upward, low_sq, high_sq))
    variant_share = lax.dynamic_slice_in_dim(
        variant_total, (samp_index % halo_shares) * share_rows, share_rows, 0
    )

    def exchange(pieces, bits):
        owners = sorted(pieces)
        arrays = [pieces[t] for t in owners]
        tags = list(owners)
        for bit in bits:
            mine = (samp_index // bit) % 2 == 1
            zeros = [i for i, t in enumerate(tags) if (t // bit) % 2 == 0]
            ones = [i for i, t in enumerate(tags) if (t // bit) % 2 == 1]
            partner = [(s, s ^ bit) for s in all_samp]
            kept = []
            for z, o in zip(zeros, ones):
                keep = jnp.where(mine, arrays[o], arrays[z])
                send = jnp.where(mine, arrays[z], arrays[o])
                kept.append(keep + lax.ppermute(send, "samp", partner))
            tags = [tags[z] for z in zeros]
            arrays = kept
        (only,) = arrays
        return only

    bits = [1 << i for i in range(samp_count.bit_length() - 2)]

    def owner_of(owners, s):
        (t,) = [t for t in owners if t % half == s % half]
        return t

    near_own = cross_rows(near_panel, phenotypes)
    far_own = cross_rows(far_panel, phenotypes)
    own_low = jnp.where(even, far_own, near_own)
    own_high = jnp.where(even, near_own, far_own)
    inner_shares = range(halo_shares, samp_count - halo_shares)
    outer_shares = [*range(halo_shares), *range(samp_count - halo_shares, samp_count)]

    def pieces_of(first, second, owners):
        out = {}
        for k, t in enumerate(owners):
            source = first if k < halo_shares else second
            row = (k % halo_shares) * share_rows
            out[t] = source[row : row + share_rows]
        return out

    own = exchange(pieces_of(own_low, own_high, inner_shares), bits)
    one_way = [(t ^ half, t) for t in inner_shares]
    own_total = own + lax.ppermute(own, "samp", one_way)

    totals = []
    for index, (low, high, rows) in enumerate(plan):
        near_edge = far_edge = None
        for (a, b), near_part, far_part in zip(rows, near[index], far[index]):
            n_part = cross_rows(near_panel[a:b], near_part)
            f_part = cross_rows(far_panel[a:b], far_part)
            near_edge = n_part if near_edge is None else near_edge + n_part
            far_edge = f_part if far_edge is None else far_edge + f_part
        up_edge = jnp.where(even, near_edge, far_edge)
        down_edge = jnp.where(even, far_edge, near_edge)
        edge = exchange(pieces_of(up_edge, down_edge, outer_shares), bits)
        shift = {t: 1 if t < half else -1 for t in outer_shares}
        straight = [
            (t, b, t, b + shift[t]) for t in outer_shares for b in all_pos if 0 <= b + shift[t] < pos_count
        ]
        across = [(t ^ half, b, t, d) for t, b, _, d in straight]
        if index < len(plan) - 1:
            edge = edge + lax.ppermute(edge, "samp", [(t ^ half, t) for t in outer_shares])
            totals.append(hop(edge, straight, pos_count))
        else:
            totals.append(hop(edge, straight, pos_count) + hop(edge, across, pos_count))
    edge_total = jnp.concatenate(totals, axis=1)
    cross_share = jnp.where(outer, edge_total, own_total)

    variant_index = (
        pos_index * block_width
        - HALO
        + samp_index * share_rows
        + jnp.arange(share_rows, dtype=jnp.int32)[:, None]
    )
    inside = (variant_index >= window_low[None, :]) & (variant_index <= window_high[None, :])
    factor = math.sqrt(float(sample_rows * samp_count - 2))
    scale_terms = (variant_share[:, None] + EPS) * (peak_total[None, :] + EPS)
    statistic = factor * cross_share / jnp.sqrt(scale_terms)
    return jnp.where(inside, statistic, jnp.zeros_like(statistic))[None]


def solution(mesh):
    placed = (P("samp", "pos"), P("samp", "pos"), P("pos"), P("pos"))
    return jax.shard_map(
        shards, mesh=mesh, in_specs=placed, out_specs=P("pos", "samp", None), check_vma=False
    )
```

```python
import functools
import math

import jax
import jax.numpy as jnp
from jax import lax
from jax.experimental import pallas as pl
from jax.experimental.pallas import tpu as pltpu
from jax.sharding import PartitionSpec as P


HALO = 512
EPS = 1e-06
LANES = 128
TAIL = 8
EARLY_SHARE = 8
EARLY_PARTS = 4
END_SHARE = 4
OWN_STEPS = 4
OWN_CALLS = 2
OWN_VMEM = 20 * 1024 * 1024


def cross_rows(variant_panel, phenotypes):
    return lax.dot_general(
        variant_panel, phenotypes, (((0,), (0,)), ((), ())), preferred_element_type=jnp.float32
    )


def added(total, part):
    return part if total is None else lax.optimization_barrier(total) + part


def folded_squares(block):
    wide = block.astype(jnp.float32)
    return jnp.sum((wide * wide).reshape(-1, 8, wide.shape[1]), axis=0)


def own_kernel(has_base, dosages, phenotypes, *refs):
    cross, variant_sq, peak_sq = refs[-3:]

    @pl.when(pl.program_id(0) == 0)
    def _():
        for index, ref in enumerate(refs[-3:]):
            ref[...] = refs[index][...] if has_base else jnp.zeros_like(ref)

    cross[...] += cross_rows(dosages[...], phenotypes[...])
    variant_sq[...] += folded_squares(dosages[...])
    peak_sq[...] += folded_squares(phenotypes[...])


def own_block(dosages, phenotypes, rows, first, count, base):
    block_width = dosages.shape[1]
    peak_width = phenotypes.shape[1]
    shapes = [(block_width, peak_width), (8, block_width), (8, peak_width)]
    sums = [pl.BlockSpec(shape, lambda i: (0, 0)) for shape in shapes]
    return pl.pallas_call(
        functools.partial(own_kernel, base is not None),
        grid=(count,),
        in_specs=[
            pl.BlockSpec((rows, block_width), lambda i: (first + i, 0)),
            pl.BlockSpec((rows, peak_width), lambda i: (first + i, 0)),
            *(sums if base else []),
        ],
        out_specs=sums,
        out_shape=[jax.ShapeDtypeStruct(shape, jnp.float32) for shape in shapes],
        compiler_params=pltpu.CompilerParams(vmem_limit_bytes=OWN_VMEM),
        name="own_block",
    )(dosages, phenotypes, *(base or ()))


def statistics_share(dosages, phenotypes, window_low, window_high):
    sample_rows, block_width = dosages.shape
    peak_width = phenotypes.shape[1]
    span_width = block_width + 2 * HALO
    samp_count = lax.axis_size("samp")
    pos_count = lax.axis_size("pos")
    samp_index = lax.axis_index("samp")
    pos_index = lax.axis_index("pos")
    share_rows = span_width // samp_count
    halo_shares = HALO // share_rows
    half = samp_count // 2
    even = pos_index % 2 == 0
    all_samp = range(samp_count)
    all_pos = range(pos_count)
    split = peak_width - LANES
    early = sample_rows * EARLY_SHARE // 16
    end = sample_rows - sample_rows * END_SHARE // 16
    step = early // EARLY_PARTS

    def hop(array, pairs):
        flat = [(a * pos_count + b, c * pos_count + d) for a, b, c, d in pairs]
        return lax.ppermute(array, ("samp", "pos"), flat)

    def parity(x, y):
        return jnp.where(even, x, y)

    swap = [(b, b ^ 1) for b in all_pos]
    onward = [(b, b + 2) for b in range(0, pos_count - 2, 2)] + [(b, b - 2) for b in range(3, pos_count, 2)]
    back = [(d, s) for s, d in onward]

    near_start = jnp.where(even, block_width - HALO, 0)
    far_start = jnp.where(even, 0, block_width - HALO)

    def half_rows(start, low, high):
        return lax.dynamic_slice(dosages, (low, start), (high - low, HALO))

    windows = [(i * step, (i + 1) * step, 0, peak_width) for i in range(EARLY_PARTS)]
    windows += [(early, sample_rows, 0, split), (early, end, split, peak_width), (end, sample_rows, split, peak_width)]
    held, source = [], phenotypes
    for i, (a, b, c, d) in enumerate(windows):
        piece = lax.slice(source, (a, c), (b, d))
        held.append(lax.ppermute(piece, "pos", swap))
        if i == 0:
            source = lax.optimization_barrier(phenotypes)
    first, left, right, tip = held[:EARLY_PARTS], *held[EARLY_PARTS:]
    passed = [lax.ppermute(x, "pos", onward) for x in first]

    far_late = lax.optimization_barrier(half_rows(far_start, early, sample_rows))
    far_in = lax.ppermute(far_late, "pos", back)

    inner_shares = list(range(halo_shares, samp_count - halo_shares))
    outer_shares = [*range(halo_shares), *range(samp_count - halo_shares, samp_count)]
    outer = (samp_index < halo_shares) | (samp_index >= samp_count - halo_shares)
    bits = [1 << i for i in range(samp_count.bit_length() - 2)]

    def rows_of(vector, width):
        block = vector.reshape(-1, width)
        return jnp.pad(block, ((0, TAIL - block.shape[0]), (0, 0)))

    def pieces_of(first, second, owners, tail):
        out = []
        for k, t in enumerate(owners):
            rows, squares = first if k < halo_shares else second
            low = (k % halo_shares) * share_rows
            high = low + share_rows
            piece = rows[low:high]
            out.append((t, jnp.concatenate([piece, tail(squares[low:high])]) if tail else piece))
        return out

    def exchange(tagged, bit):
        mine = (samp_index // bit) % 2 == 1
        zeros = [x for x in tagged if (x[0] // bit) % 2 == 0]
        ones = [x for x in tagged if (x[0] // bit) % 2 == 1]
        kept = []
        for (tag, z), (_, o) in zip(zeros, ones):
            keep, send = jnp.where(mine, o, z), jnp.where(mine, z, o)
            kept.append((tag, keep + lax.ppermute(send, "samp", [(s, s ^ bit) for s in all_samp])))
        return kept

    own = None
    for i in range(OWN_CALLS):
        count = OWN_STEPS // OWN_CALLS
        own = own_block(dosages, phenotypes, sample_rows // OWN_STEPS, i * count, count, own)
    own, own_sq, peak_sq = own
    own_sq, peak_sq = jnp.sum(own_sq, axis=0), jnp.sum(peak_sq, axis=0)
    low_sq, high_sq = own_sq[:HALO], own_sq[block_width - HALO :]
    near_sq, far_sq = parity(high_sq, low_sq), parity(low_sq, high_sq)

    def own_tail(sums):
        return jnp.concatenate([rows_of(sums, split), rows_of(peak_sq, LANES)], axis=1)

    own = pieces_of((own[:HALO], low_sq), (own[block_width - HALO :], high_sq), inner_shares, own_tail)
    for bit in bits:
        own = exchange(own, bit)
    ((_, own),) = own
    own_total = own + lax.ppermute(own, "samp", [(t ^ half, t) for t in inner_shares])
    peak_total = own[share_rows:, split:]
    peak_total = peak_total + lax.ppermute(peak_total, "samp", [(s, s ^ half) for s in all_samp])
    peak_total = peak_total[: peak_width // LANES].reshape(peak_width)

    near_early = cross_rows(half_rows(near_start, 0, early), jnp.concatenate(first))
    far_early = cross_rows(half_rows(far_start, 0, early - step), jnp.concatenate(passed[:-1]))
    far_early = added(far_early, cross_rows(half_rows(far_start, early - step, early), passed[-1]))

    def acc_tail(sums):
        return jnp.pad(rows_of(sums, split), ((0, 0), (0, LANES)))

    acc = pieces_of(
        (parity(0.0, far_early), parity(0.0, far_sq)),
        (parity(far_early, 0.0), parity(far_sq, 0.0)),
        outer_shares,
        acc_tail,
    )
    acc = exchange(acc, 1)
    acc_pairs = [(s, b, s, d) for s in all_samp for b, d in back if halo_shares > 1 or (s + b) % 2 == 1]
    acc = [hop(x, acc_pairs) for _, x in acc]

    straight = [(t, b, t, b ^ 1) for t in outer_shares for b in all_pos]
    across = [(t ^ half, b, t, b ^ 1) for t in outer_shares for b in all_pos]

    def reduced(pieces, low, high):
        pieces = exchange(pieces, 1)
        pieces = [(t, x + y[: x.shape[0], low:high]) for (t, x), y in zip(pieces, acc)]
        for bit in bits[1:]:
            pieces = exchange(pieces, bit)
        ((_, only),) = pieces
        return only

    near_edge = near_early[:, :split] + cross_rows(half_rows(near_start, early, sample_rows), left)
    far_edge = cross_rows(far_in, left)
    up, down = parity(near_edge, far_edge), parity(far_edge, near_edge)
    none = jnp.zeros_like(near_sq)
    pieces = pieces_of(
        (up, parity(near_sq, none)),
        (down, parity(none, near_sq)),
        outer_shares,
        lambda sums: rows_of(sums, split),
    )
    edge = reduced(pieces, 0, split)
    left_total = hop(edge, straight) + hop(edge, across)

    near_edge = near_early[:, split:] + cross_rows(half_rows(near_start, early, end), right)
    far_edge = cross_rows(far_in[: end - early], right)
    near_edge = added(near_edge, cross_rows(half_rows(near_start, end, sample_rows), tip))
    far_edge = added(far_edge, cross_rows(far_in[end - early :], tip))
    up, down = parity(near_edge, far_edge), parity(far_edge, near_edge)
    pieces = pieces_of((up, near_sq), (down, near_sq), outer_shares, None)
    edge = reduced(pieces, split, peak_width)
    right_total = hop(edge, straight) + hop(edge, across)

    left_share = jnp.where(outer, left_total, own_total[:, :split])
    right_share = jnp.where(outer, right_total, own_total[:share_rows, split:])
    variant_share = left_share[share_rows : share_rows + share_rows // split].reshape(share_rows)
    cross_share = jnp.concatenate([left_share[:share_rows], right_share], axis=1)

    variant_index = (
        pos_index * block_width
        - HALO
        + samp_index * share_rows
        + jnp.arange(share_rows, dtype=jnp.int32)[:, None]
    )
    inside = (variant_index >= window_low[None, :]) & (variant_index <= window_high[None, :])
    factor = math.sqrt(float(sample_rows * samp_count - 2))
    scale_terms = (variant_share[:, None] + EPS) * (peak_total[None, :] + EPS)
    statistic = factor * cross_share / jnp.sqrt(scale_terms)
    return jnp.where(inside, statistic, jnp.zeros_like(statistic))[None]


def solution(mesh):
    placed = (P("samp", "pos"), P("samp", "pos"), P("pos"), P("pos"))
    return jax.shard_map(
        statistics_share, mesh=mesh, in_specs=placed, out_specs=P("pos", "samp", None), check_vma=False
    )
```

```python
import functools
import math

import jax
import jax.numpy as jnp
from jax import lax
from jax.experimental import pallas as pl
from jax.experimental.pallas import tpu as pltpu
from jax.sharding import PartitionSpec as P


HALO = 512
EPS = 1e-06
LANES = 128
TAIL = 8
EARLY_SHARE = 8
EARLY_PARTS = 4
END_SHARE = 2
GROUP_TILES = (2,)
X_STAGE = False
OWN_CALLS = 2
OWN_STEPS = 4
OWN_VMEM = 20 * 1024 * 1024


def cross_rows(variant_panel, phenotypes):
    return lax.dot_general(
        variant_panel, phenotypes, (((0,), (0,)), ((), ())), preferred_element_type=jnp.float32
    )


def added(total, part):
    return part if total is None else lax.optimization_barrier(total) + part


def folded_squares(block):
    wide = block.astype(jnp.float32)
    return jnp.sum((wide * wide).reshape(-1, 8, wide.shape[1]), axis=0)


def own_kernel(share_rows, dosages, phenotypes, *refs):
    (*pieces, tails), (cross, variant_sq, peak_sq) = refs[:-3], refs[-3:]
    split = tails.shape[1]
    last = phenotypes.shape[1] - LANES

    @pl.when(pl.program_id(0) == 0)
    def _():
        for ref in (cross, variant_sq, peak_sq):
            ref[...] = jnp.zeros_like(ref)

    cross[...] += cross_rows(dosages[...], phenotypes[...])
    variant_sq[...] += folded_squares(dosages[...])
    peak_sq[...] += folded_squares(phenotypes[...])

    @pl.when(pl.program_id(0) == pl.num_programs(0) - 1)
    def _():
        variant_sums = jnp.sum(variant_sq[...], axis=0, keepdims=True)
        peak_sums = jnp.sum(peak_sq[...], axis=0, keepdims=True)
        tails[...] = jnp.zeros_like(tails)
        for k, piece in enumerate(pieces):
            first = k * share_rows
            piece[:share_rows] = cross[first : first + share_rows]
            piece[share_rows:] = jnp.zeros((TAIL, piece.shape[1]), jnp.float32)
            for row in range(share_rows // split):
                sums = variant_sums[:, first + row * split : first + (row + 1) * split]
                piece[share_rows + row : share_rows + row + 1, :split] = sums
                tails[k * TAIL + row : k * TAIL + row + 1] = sums
            for row in range(peak_sums.shape[1] // LANES):
                sums = peak_sums[:, row * LANES : (row + 1) * LANES]
                piece[share_rows + row : share_rows + row + 1, last:] = sums


def own_block(dosages, phenotypes, share_rows, split, part):
    sample_rows, block_width = dosages.shape
    peak_width = phenotypes.shape[1]
    rows = sample_rows // OWN_STEPS
    shares = block_width // share_rows
    steps = OWN_STEPS // OWN_CALLS
    shapes = [(share_rows + TAIL, peak_width)] * shares + [(shares * TAIL, split)]
    return pl.pallas_call(
        functools.partial(own_kernel, share_rows),
        grid=(steps,),
        in_specs=[
            pl.BlockSpec((rows, block_width), lambda i: (part * steps + i, 0)),
            pl.BlockSpec((rows, peak_width), lambda i: (part * steps + i, 0)),
        ],
        out_specs=[pl.BlockSpec(shape, lambda i: (0, 0)) for shape in shapes],
        out_shape=[jax.ShapeDtypeStruct(shape, jnp.float32) for shape in shapes],
        scratch_shapes=[
            pltpu.VMEM((block_width, peak_width), jnp.float32),
            pltpu.VMEM((8, block_width), jnp.float32),
            pltpu.VMEM((8, peak_width), jnp.float32),
        ],
        compiler_params=pltpu.CompilerParams(vmem_limit_bytes=OWN_VMEM),
        name="own_block",
    )(dosages, phenotypes)


def statistics_share(dosages, phenotypes, window_low, window_high):
    sample_rows, block_width = dosages.shape
    peak_width = phenotypes.shape[1]
    span_width = block_width + 2 * HALO
    samp_count = lax.axis_size("samp")
    pos_count = lax.axis_size("pos")
    samp_index = lax.axis_index("samp")
    pos_index = lax.axis_index("pos")
    share_rows = span_width // samp_count
    halo_shares = HALO // share_rows
    half = samp_count // 2
    all_samp = range(samp_count)
    all_pos = range(pos_count)
    ends = [0]
    for tiles in GROUP_TILES:
        ends.append(ends[-1] + tiles * LANES)
    groups = list(zip(ends, [*ends[1:], peak_width]))
    early = sample_rows * EARLY_SHARE // 16
    end = sample_rows - sample_rows * END_SHARE // 16
    step = early // EARLY_PARTS

    even = (pos_index & 1) == 0
    near_start = jnp.where(even, block_width - HALO, 0)
    far_start = jnp.where(even, 0, block_width - HALO)
    outer = (samp_index < halo_shares) | (samp_index >= samp_count - halo_shares)
    odd_at = [(samp_index & (1 << i)) != 0 for i in range(samp_count.bit_length() - 2)]
    first_variant = pos_index * block_width - HALO + samp_index * share_rows
    dosages, phenotypes, even, near_start, far_start, outer, odd_at, first_variant = lax.optimization_barrier(
        (dosages, phenotypes, even, near_start, far_start, outer, odd_at, first_variant)
    )

    def hop(array, pairs):
        flat = [(a * pos_count + b, c * pos_count + d) for a, b, c, d in pairs]
        return lax.ppermute(array, ("samp", "pos"), flat)

    def parity(x, y):
        return jnp.where(even, x, y)

    swap = [(b, b ^ 1) for b in all_pos]
    onward = [(b, b + 2) for b in range(0, pos_count - 2, 2)] + [(b, b - 2) for b in range(3, pos_count, 2)]
    back = [(d, s) for s, d in onward]

    def half_rows(start, low, high):
        return lax.dynamic_slice(dosages, (low, start), (high - low, HALO), allow_negative_indices=False)

    windows = [(i * step, (i + 1) * step, 0, peak_width) for i in range(EARLY_PARTS)]
    windows += [(early, sample_rows, low, high) for low, high in groups[:-1]]
    windows += [(early, end, ends[-1], peak_width), (end, sample_rows, ends[-1], peak_width)]
    held, source = [], phenotypes
    for i, (a, b, c, d) in enumerate(windows):
        piece = lax.slice(source, (a, c), (b, d))
        held.append(lax.ppermute(piece, "pos", swap))
        if i == 0:
            source = lax.optimization_barrier(phenotypes)
    first, late, right, tip = held[:EARLY_PARTS], held[EARLY_PARTS:-2], held[-2], held[-1]
    passed = [lax.ppermute(x, "pos", onward) for x in first]

    far_late = lax.optimization_barrier(half_rows(far_start, early, sample_rows))
    far_in = lax.ppermute(far_late, "pos", back)

    inner_shares = list(range(halo_shares, samp_count - halo_shares))
    outer_shares = [*range(halo_shares), *range(samp_count - halo_shares, samp_count)]
    bits = [1 << i for i in range(samp_count.bit_length() - 2)]

    def pieces_of(first, second, owners):
        out = []
        for k, t in enumerate(owners):
            rows, tails = first if k < halo_shares else second
            low = (k % halo_shares) * share_rows
            piece = rows[low : low + share_rows]
            out.append((t, jnp.concatenate([piece, tails[k % halo_shares]]) if tails else piece))
        return out

    def exchange(tagged, bit):
        mine = odd_at[bit.bit_length() - 1]
        zeros = [x for x in tagged if (x[0] // bit) % 2 == 0]
        ones = [x for x in tagged if (x[0] // bit) % 2 == 1]
        kept = []
        for (tag, z), (_, o) in zip(zeros, ones):
            keep, send = jnp.where(mine, o, z), jnp.where(mine, z, o)
            kept.append((tag, keep + lax.ppermute(send, "samp", [(s, s ^ bit) for s in all_samp])))
        return kept

    parts = []
    for part in range(OWN_CALLS):
        parts.append(own_block(dosages, phenotypes, share_rows, groups[0][1], part))
    *own, tails = [sum(x[1:], x[0]) for x in zip(*parts)]
    tails = [tails[k * TAIL : (k + 1) * TAIL] for k in range(len(own))]
    own = list(zip(inner_shares, own))
    low_tails, high_tails = tails[:halo_shares], tails[-halo_shares:]
    near_tails = [parity(h, l) for h, l in zip(high_tails, low_tails)]
    far_tails = [parity(l, h) for h, l in zip(high_tails, low_tails)]
    for bit in bits:
        own = exchange(own, bit)
    ((_, own),) = own
    own_total = own + lax.ppermute(own, "samp", [(t ^ half, t) for t in inner_shares])
    peak_total = jnp.maximum(own[share_rows:, peak_width - LANES :], 0.0)
    peak_total = peak_total + lax.ppermute(peak_total, "samp", [(s, s ^ half) for s in all_samp])
    peak_total = peak_total[: peak_width // LANES].reshape(peak_width)

    near_early = cross_rows(half_rows(near_start, 0, early), jnp.concatenate(first))
    far_early = cross_rows(half_rows(far_start, 0, early - step), jnp.concatenate(passed[:-1]))
    far_early = added(far_early, cross_rows(half_rows(far_start, early - step, early), passed[-1]))

    wide = [jnp.pad(x, ((0, 0), (0, peak_width - x.shape[1]))) for x in far_tails]
    acc = pieces_of(
        (parity(0.0, far_early), [parity(0.0, x) for x in wide]),
        (parity(far_early, 0.0), [parity(x, 0.0) for x in wide]),
        outer_shares,
    )
    acc = exchange(acc, 1)
    acc_pairs = [(s, b, s, d) for s in all_samp for b, d in back if halo_shares > 1 or (s + b) % 2 == 1]
    acc = [hop(x, acc_pairs) for _, x in acc]

    straight = [(t, b, t, b ^ 1) for t in outer_shares for b in all_pos]
    across = [(t ^ half, b, t, b ^ 1) for t in outer_shares for b in all_pos]

    def reduced(pieces, low, high):
        pieces = exchange(pieces, 1)
        pieces = [(t, x + y[: x.shape[0], low:high]) for (t, x), y in zip(pieces, acc)]
        for bit in bits[1:]:
            pieces = exchange(pieces, bit)
        ((_, only),) = pieces
        return only

    totals = []
    for g, ((low, high), peaks) in enumerate(zip(groups, late)):
        near_edge = near_early[:, low:high] + cross_rows(half_rows(near_start, early, sample_rows), peaks)
        far_edge = cross_rows(far_in, peaks)
        up, down = parity(near_edge, far_edge), parity(far_edge, near_edge)
        up_tails = [parity(x, 0.0) for x in near_tails] if g == 0 else None
        down_tails = [parity(0.0, x) for x in near_tails] if g == 0 else None
        edge = reduced(pieces_of((up, up_tails), (down, down_tails), outer_shares), low, high)
        if X_STAGE:
            edge = edge + lax.ppermute(edge, "samp", [(t ^ half, t) for t in outer_shares])
            totals.append(hop(edge, straight))
        else:
            totals.append(hop(edge, straight) + hop(edge, across))

    low, high = groups[-1]
    near_edge = near_early[:, low:high] + cross_rows(half_rows(near_start, early, end), right)
    far_edge = cross_rows(far_in[: end - early], right)
    near_edge = added(near_edge, cross_rows(half_rows(near_start, end, sample_rows), tip))
    far_edge = added(far_edge, cross_rows(far_in[end - early :], tip))
    up, down = parity(near_edge, far_edge), parity(far_edge, near_edge)
    edge = reduced(pieces_of((up, None), (down, None), outer_shares), low, high)
    totals.append(hop(edge, straight) + hop(edge, across))

    shares = [
        jnp.where(outer, total, own_total[: total.shape[0], low:high]) for total, (low, high) in zip(totals, groups)
    ]
    split = groups[0][1]
    variant_share = shares[0][share_rows : share_rows + share_rows // split].reshape(share_rows)
    cross_share = jnp.concatenate([x[:share_rows] for x in shares], axis=1)

    variant_index = first_variant + jnp.arange(share_rows, dtype=jnp.int32)[:, None]
    inside = (variant_index >= window_low[None, :]) & (variant_index <= window_high[None, :])
    factor = math.sqrt(float(sample_rows * samp_count - 2))
    scale_terms = (variant_share[:, None] + EPS) * (peak_total[None, :] + EPS)
    statistic = factor * cross_share / jnp.sqrt(scale_terms)
    return jnp.where(inside, statistic, jnp.zeros_like(statistic))[None]


def solution(mesh):
    placed = (P("samp", "pos"), P("samp", "pos"), P("pos"), P("pos"))
    return jax.shard_map(
        statistics_share, mesh=mesh, in_specs=placed, out_specs=P("pos", "samp", None), check_vma=False
    )
```

```python
import functools
import math

import jax
import jax.numpy as jnp
from jax import lax
from jax.experimental import pallas as pl
from jax.experimental.pallas import tpu as pltpu
from jax.sharding import PartitionSpec as P


HALO = 512
EPS = 1e-06
LANES = 128
TAIL = 8
EARLY_SHARE = 8
EARLY_PARTS = 4
END_SHARE = 2
GROUP_TILES = (2,)
X_STAGE = False
OWN_CALLS = 2
DIRECT_CUTS = 2
COPY_STEPS = 4
COPY_VMEM = 8 * 1024 * 1024
OWN_STEPS = 4
OWN_VMEM = 20 * 1024 * 1024


def cross_rows(variant_panel, phenotypes):
    return lax.dot_general(
        variant_panel, phenotypes, (((0,), (0,)), ((), ())), preferred_element_type=jnp.float32
    )


def added(total, part):
    return part if total is None else lax.optimization_barrier(total) + part


def folded_squares(block):
    wide = block.astype(jnp.float32)
    return jnp.sum((wide * wide).reshape(-1, 8, wide.shape[1]), axis=0)


def copy_kernel(source, copy):
    copy[...] = source[...]


def near_copy(array):
    rows = array.shape[0] // COPY_STEPS
    block = pl.BlockSpec((rows, array.shape[1]), lambda i: (i, 0))
    return pl.pallas_call(
        copy_kernel,
        grid=(COPY_STEPS,),
        in_specs=[block],
        out_specs=block,
        out_shape=jax.ShapeDtypeStruct(array.shape, array.dtype),
        compiler_params=pltpu.CompilerParams(vmem_limit_bytes=COPY_VMEM),
    )(array)


def own_kernel(share_rows, dosages, phenotypes, *refs):
    (*pieces, tails), (cross, variant_sq, peak_sq) = refs[:-3], refs[-3:]
    split = tails.shape[1]
    last = phenotypes.shape[1] - LANES

    @pl.when(pl.program_id(0) == 0)
    def _():
        for ref in (cross, variant_sq, peak_sq):
            ref[...] = jnp.zeros_like(ref)

    cross[...] += cross_rows(dosages[...], phenotypes[...])
    variant_sq[...] += folded_squares(dosages[...])
    peak_sq[...] += folded_squares(phenotypes[...])

    @pl.when(pl.program_id(0) == pl.num_programs(0) - 1)
    def _():
        variant_sums = jnp.sum(variant_sq[...], axis=0, keepdims=True)
        peak_sums = jnp.sum(peak_sq[...], axis=0, keepdims=True)
        tails[...] = jnp.zeros_like(tails)
        for k, piece in enumerate(pieces):
            first = k * share_rows
            piece[:share_rows] = cross[first : first + share_rows]
            piece[share_rows:] = jnp.zeros((TAIL, piece.shape[1]), jnp.float32)
            for row in range(share_rows // split):
                sums = variant_sums[:, first + row * split : first + (row + 1) * split]
                piece[share_rows + row : share_rows + row + 1, :split] = sums
                tails[k * TAIL + row : k * TAIL + row + 1] = sums
            for row in range(peak_sums.shape[1] // LANES):
                sums = peak_sums[:, row * LANES : (row + 1) * LANES]
                piece[share_rows + row : share_rows + row + 1, last:] = sums


def own_block(dosages, phenotypes, share_rows, split, part):
    sample_rows, block_width = dosages.shape
    peak_width = phenotypes.shape[1]
    rows = sample_rows // OWN_STEPS
    shares = block_width // share_rows
    steps = OWN_STEPS // OWN_CALLS
    shapes = [(share_rows + TAIL, peak_width)] * shares + [(shares * TAIL, split)]
    return pl.pallas_call(
        functools.partial(own_kernel, share_rows),
        grid=(steps,),
        in_specs=[
            pl.BlockSpec((rows, block_width), lambda i: (part * steps + i, 0)),
            pl.BlockSpec((rows, peak_width), lambda i: (part * steps + i, 0)),
        ],
        out_specs=[pl.BlockSpec(shape, lambda i: (0, 0)) for shape in shapes],
        out_shape=[jax.ShapeDtypeStruct(shape, jnp.float32) for shape in shapes],
        scratch_shapes=[
            pltpu.VMEM((block_width, peak_width), jnp.float32),
            pltpu.VMEM((8, block_width), jnp.float32),
            pltpu.VMEM((8, peak_width), jnp.float32),
        ],
        compiler_params=pltpu.CompilerParams(vmem_limit_bytes=OWN_VMEM),
        name="own_block",
    )(dosages, phenotypes)


def statistics_share(dosages, phenotypes, window_low, window_high):
    sample_rows, block_width = dosages.shape
    peak_width = phenotypes.shape[1]
    span_width = block_width + 2 * HALO
    samp_count = lax.axis_size("samp")
    pos_count = lax.axis_size("pos")
    samp_index = lax.axis_index("samp")
    pos_index = lax.axis_index("pos")
    share_rows = span_width // samp_count
    halo_shares = HALO // share_rows
    half = samp_count // 2
    all_samp = range(samp_count)
    all_pos = range(pos_count)
    ends = [0]
    for tiles in GROUP_TILES:
        ends.append(ends[-1] + tiles * LANES)
    groups = list(zip(ends, [*ends[1:], peak_width]))
    early = sample_rows * EARLY_SHARE // 16
    end = sample_rows - sample_rows * END_SHARE // 16
    step = early // EARLY_PARTS

    even = (pos_index & 1) == 0
    near_start = jnp.where(even, block_width - HALO, 0)
    far_start = jnp.where(even, 0, block_width - HALO)
    outer = (samp_index < halo_shares) | (samp_index >= samp_count - halo_shares)
    odd_at = [(samp_index & (1 << i)) != 0 for i in range(samp_count.bit_length() - 2)]
    first_variant = pos_index * block_width - HALO + samp_index * share_rows
    dosages, phenotypes, even, near_start, far_start, outer, odd_at, first_variant = lax.optimization_barrier(
        (dosages, phenotypes, even, near_start, far_start, outer, odd_at, first_variant)
    )

    def hop(array, pairs):
        flat = [(a * pos_count + b, c * pos_count + d) for a, b, c, d in pairs]
        return lax.ppermute(array, ("samp", "pos"), flat)

    def parity(x, y):
        return jnp.where(even, x, y)

    swap = [(b, b ^ 1) for b in all_pos]
    onward = [(b, b + 2) for b in range(0, pos_count - 2, 2)] + [(b, b - 2) for b in range(3, pos_count, 2)]
    back = [(d, s) for s, d in onward]

    def half_rows(start, low, high):
        return lax.dynamic_slice(dosages, (low, start), (high - low, HALO), allow_negative_indices=False)

    windows = [(i * step, (i + 1) * step, 0, peak_width) for i in range(EARLY_PARTS)]
    windows += [(early, sample_rows, low, high) for low, high in groups[:-1]]
    windows += [(early, end, ends[-1], peak_width), (end, sample_rows, ends[-1], peak_width)]
    held, source = [], phenotypes
    phenotypes = near_copy(phenotypes)
    for i, (a, b, c, d) in enumerate(windows):
        piece = lax.slice(source, (a, c), (b, d))
        held.append(lax.ppermute(piece, "pos", swap))
        if i == DIRECT_CUTS - 1:
            source = phenotypes
    first, late, right, tip = held[:EARLY_PARTS], held[EARLY_PARTS:-2], held[-2], held[-1]
    passed = [lax.ppermute(x, "pos", onward) for x in first]

    far_late = lax.optimization_barrier(half_rows(far_start, early, sample_rows))
    far_in = lax.ppermute(far_late, "pos", back)

    inner_shares = list(range(halo_shares, samp_count - halo_shares))
    outer_shares = [*range(halo_shares), *range(samp_count - halo_shares, samp_count)]
    bits = [1 << i for i in range(samp_count.bit_length() - 2)]

    def pieces_of(first, second, owners):
        out = []
        for k, t in enumerate(owners):
            rows, tails = first if k < halo_shares else second
            low = (k % halo_shares) * share_rows
            piece = rows[low : low + share_rows]
            out.append((t, jnp.concatenate([piece, tails[k % halo_shares]]) if tails else piece))
        return out

    def exchange(tagged, bit):
        mine = odd_at[bit.bit_length() - 1]
        zeros = [x for x in tagged if (x[0] // bit) % 2 == 0]
        ones = [x for x in tagged if (x[0] // bit) % 2 == 1]
        kept = []
        for (tag, z), (_, o) in zip(zeros, ones):
            keep, send = jnp.where(mine, o, z), jnp.where(mine, z, o)
            kept.append((tag, keep + lax.ppermute(send, "samp", [(s, s ^ bit) for s in all_samp])))
        return kept

    parts = []
    for part in range(OWN_CALLS):
        parts.append(own_block(dosages, phenotypes, share_rows, groups[0][1], part))
    *own, tails = [sum(x[1:], x[0]) for x in zip(*parts)]
    tails = [tails[k * TAIL : (k + 1) * TAIL] for k in range(len(own))]
    own = list(zip(inner_shares, own))
    low_tails, high_tails = tails[:halo_shares], tails[-halo_shares:]
    near_tails = [parity(h, l) for h, l in zip(high_tails, low_tails)]
    far_tails = [parity(l, h) for h, l in zip(high_tails, low_tails)]
    for bit in bits:
        own = exchange(own, bit)
    ((_, own),) = own
    own_total = own + lax.ppermute(own, "samp", [(t ^ half, t) for t in inner_shares])
    peak_total = jnp.maximum(own[share_rows:, peak_width - LANES :], 0.0)
    peak_total = peak_total + lax.ppermute(peak_total, "samp", [(s, s ^ half) for s in all_samp])
    peak_total = peak_total[: peak_width // LANES].reshape(peak_width)

    near_early = cross_rows(half_rows(near_start, 0, early), jnp.concatenate(first))
    far_early = cross_rows(half_rows(far_start, 0, early - step), jnp.concatenate(passed[:-1]))
    far_early = added(far_early, cross_rows(half_rows(far_start, early - step, early), passed[-1]))

    wide = [jnp.pad(x, ((0, 0), (0, peak_width - x.shape[1]))) for x in far_tails]
    acc = pieces_of(
        (parity(0.0, far_early), [parity(0.0, x) for x in wide]),
        (parity(far_early, 0.0), [parity(x, 0.0) for x in wide]),
        outer_shares,
    )
    acc = exchange(acc, 1)
    acc_pairs = [(s, b, s, d) for s in all_samp for b, d in back if halo_shares > 1 or (s + b) % 2 == 1]
    acc = [hop(x, acc_pairs) for _, x in acc]

    straight = [(t, b, t, b ^ 1) for t in outer_shares for b in all_pos]
    across = [(t ^ half, b, t, b ^ 1) for t in outer_shares for b in all_pos]

    def reduced(pieces, low, high):
        pieces = exchange(pieces, 1)
        pieces = [(t, x + y[: x.shape[0], low:high]) for (t, x), y in zip(pieces, acc)]
        for bit in bits[1:]:
            pieces = exchange(pieces, bit)
        ((_, only),) = pieces
        return only

    totals = []
    for g, ((low, high), peaks) in enumerate(zip(groups, late)):
        near_edge = near_early[:, low:high] + cross_rows(half_rows(near_start, early, sample_rows), peaks)
        far_edge = cross_rows(far_in, peaks)
        up, down = parity(near_edge, far_edge), parity(far_edge, near_edge)
        up_tails = [parity(x, 0.0) for x in near_tails] if g == 0 else None
        down_tails = [parity(0.0, x) for x in near_tails] if g == 0 else None
        edge = reduced(pieces_of((up, up_tails), (down, down_tails), outer_shares), low, high)
        if X_STAGE:
            edge = edge + lax.ppermute(edge, "samp", [(t ^ half, t) for t in outer_shares])
            totals.append(hop(edge, straight))
        else:
            totals.append(hop(edge, straight) + hop(edge, across))

    low, high = groups[-1]
    near_edge = near_early[:, low:high] + cross_rows(half_rows(near_start, early, end), right)
    far_edge = cross_rows(far_in[: end - early], right)
    near_edge = added(near_edge, cross_rows(half_rows(near_start, end, sample_rows), tip))
    far_edge = added(far_edge, cross_rows(far_in[end - early :], tip))
    up, down = parity(near_edge, far_edge), parity(far_edge, near_edge)
    edge = reduced(pieces_of((up, None), (down, None), outer_shares), low, high)
    totals.append(hop(edge, straight) + hop(edge, across))

    shares = [
        jnp.where(outer, total, own_total[: total.shape[0], low:high]) for total, (low, high) in zip(totals, groups)
    ]
    split = groups[0][1]
    variant_share = shares[0][share_rows : share_rows + share_rows // split].reshape(share_rows)
    variant_index = first_variant + jnp.arange(share_rows, dtype=jnp.int32)[:, None]
    factor = math.sqrt(float(sample_rows * samp_count - 2))

    def statistic_of(cross_share, low, high):
        lows, highs = window_low[None, low:high], window_high[None, low:high]
        inside = (variant_index >= lows) & (variant_index <= highs)
        scale_terms = (variant_share[:, None] + EPS) * (peak_total[None, low:high] + EPS)
        statistic = factor * cross_share / jnp.sqrt(scale_terms)
        return jnp.where(inside, statistic, jnp.zeros_like(statistic))

    head = [statistic_of(x[:share_rows], *group) for x, group in zip(shares[:-1], groups)]
    head = jnp.pad(jnp.concatenate(head, axis=1), ((0, 0), (0, peak_width - ends[-1])))
    head = lax.optimization_barrier(head)
    return lax.dynamic_update_slice(head, statistic_of(shares[-1][:share_rows], *groups[-1]), (0, ends[-1]))[None]


def solution(mesh):
    placed = (P("samp", "pos"), P("samp", "pos"), P("pos"), P("pos"))
    return jax.shard_map(
        statistics_share, mesh=mesh, in_specs=placed, out_specs=P("pos", "samp", None), check_vma=False
    )
```

```python
import functools
import math

import jax
import jax.numpy as jnp
from jax import lax
from jax.experimental import pallas as pl
from jax.experimental.pallas import tpu as pltpu
from jax.sharding import PartitionSpec as P


HALO = 512
EPS = 1e-06
LANES = 128
TAIL = 8
EARLY_SHARE = 8
EARLY_PARTS = 4
END_SHARE = 2
GROUP_TILES = (2,)
OWN_CALLS = 2
DIRECT_CUTS = 2
COPY_STEPS = 4
COPY_VMEM = 8 * 1024 * 1024
OWN_STEPS = 4
OWN_VMEM = 20 * 1024 * 1024


def cross_rows(variant_panel, phenotypes):
    return lax.dot_general(
        variant_panel, phenotypes, (((0,), (0,)), ((), ())), preferred_element_type=jnp.float32
    )


def added(total, part):
    return part if total is None else lax.optimization_barrier(total) + part


def folded_squares(block):
    wide = block.astype(jnp.float32)
    return jnp.sum((wide * wide).reshape(-1, 8, wide.shape[1]), axis=0)


def copy_kernel(source, copy):
    copy[...] = source[...]


def near_copy(array):
    rows = array.shape[0] // COPY_STEPS
    block = pl.BlockSpec((rows, array.shape[1]), lambda i: (i, 0))
    return pl.pallas_call(
        copy_kernel,
        grid=(COPY_STEPS,),
        in_specs=[block],
        out_specs=block,
        out_shape=jax.ShapeDtypeStruct(array.shape, array.dtype),
        compiler_params=pltpu.CompilerParams(vmem_limit_bytes=COPY_VMEM),
    )(array)


def own_kernel(share_rows, dosages, phenotypes, *refs):
    (*pieces, tails), (cross, variant_sq, peak_sq) = refs[:-3], refs[-3:]
    split = tails.shape[1]
    last = phenotypes.shape[1] - LANES

    @pl.when(pl.program_id(0) == 0)
    def _():
        for ref in (cross, variant_sq, peak_sq):
            ref[...] = jnp.zeros_like(ref)

    cross[...] += cross_rows(dosages[...], phenotypes[...])
    variant_sq[...] += folded_squares(dosages[...])
    peak_sq[...] += folded_squares(phenotypes[...])

    @pl.when(pl.program_id(0) == pl.num_programs(0) - 1)
    def _():
        variant_sums = jnp.sum(variant_sq[...], axis=0, keepdims=True)
        peak_sums = jnp.sum(peak_sq[...], axis=0, keepdims=True)
        tails[...] = jnp.zeros_like(tails)
        for k, piece in enumerate(pieces):
            first = k * share_rows
            piece[:share_rows] = cross[first : first + share_rows]
            piece[share_rows:] = jnp.zeros((TAIL, piece.shape[1]), jnp.float32)
            for row in range(share_rows // split):
                sums = variant_sums[:, first + row * split : first + (row + 1) * split]
                piece[share_rows + row : share_rows + row + 1, :split] = sums
                tails[k * TAIL + row : k * TAIL + row + 1] = sums
            for row in range(peak_sums.shape[1] // LANES):
                sums = peak_sums[:, row * LANES : (row + 1) * LANES]
                piece[share_rows + row : share_rows + row + 1, last:] = sums


def own_block(dosages, phenotypes, share_rows, split, part):
    sample_rows, block_width = dosages.shape
    peak_width = phenotypes.shape[1]
    rows = sample_rows // OWN_STEPS
    shares = block_width // share_rows
    steps = OWN_STEPS // OWN_CALLS
    shapes = [(share_rows + TAIL, peak_width)] * shares + [(shares * TAIL, split)]
    return pl.pallas_call(
        functools.partial(own_kernel, share_rows),
        grid=(steps,),
        in_specs=[
            pl.BlockSpec((rows, block_width), lambda i: (part * steps + i, 0)),
            pl.BlockSpec((rows, peak_width), lambda i: (part * steps + i, 0)),
        ],
        out_specs=[pl.BlockSpec(shape, lambda i: (0, 0)) for shape in shapes],
        out_shape=[jax.ShapeDtypeStruct(shape, jnp.float32) for shape in shapes],
        scratch_shapes=[
            pltpu.VMEM((block_width, peak_width), jnp.float32),
            pltpu.VMEM((8, block_width), jnp.float32),
            pltpu.VMEM((8, peak_width), jnp.float32),
        ],
        compiler_params=pltpu.CompilerParams(vmem_limit_bytes=OWN_VMEM),
        name="own_block",
    )(dosages, phenotypes)


def statistics_share(dosages, phenotypes, window_low, window_high):
    sample_rows, block_width = dosages.shape
    peak_width = phenotypes.shape[1]
    span_width = block_width + 2 * HALO
    samp_count = lax.axis_size("samp")
    pos_count = lax.axis_size("pos")
    samp_index = lax.axis_index("samp")
    pos_index = lax.axis_index("pos")
    share_rows = span_width // samp_count
    halo_shares = HALO // share_rows
    half = samp_count // 2
    all_samp = range(samp_count)
    all_pos = range(pos_count)
    ends = [0]
    for tiles in GROUP_TILES:
        ends.append(ends[-1] + tiles * LANES)
    groups = list(zip(ends, [*ends[1:], peak_width]))
    early = sample_rows * EARLY_SHARE // 16
    end = sample_rows - sample_rows * END_SHARE // 16
    step = early // EARLY_PARTS

    even = (pos_index & 1) == 0
    near_start = jnp.where(even, block_width - HALO, 0)
    far_start = jnp.where(even, 0, block_width - HALO)
    outer = (samp_index < halo_shares) | (samp_index >= samp_count - halo_shares)
    odd_at = [(samp_index & (1 << i)) != 0 for i in range(samp_count.bit_length() - 2)]
    first_variant = pos_index * block_width - HALO + samp_index * share_rows
    dosages, phenotypes, even, near_start, far_start, outer, odd_at, first_variant = lax.optimization_barrier(
        (dosages, phenotypes, even, near_start, far_start, outer, odd_at, first_variant)
    )

    def hop(array, pairs):
        flat = [(a * pos_count + b, c * pos_count + d) for a, b, c, d in pairs]
        return lax.ppermute(array, ("samp", "pos"), flat)

    def parity(x, y):
        return jnp.where(even, x, y)

    swap = [(b, b ^ 1) for b in all_pos]
    onward = [(b, b + 2) for b in range(0, pos_count - 2, 2)] + [(b, b - 2) for b in range(3, pos_count, 2)]
    back = [(d, s) for s, d in onward]

    def half_rows(start, low, high):
        return lax.dynamic_slice(dosages, (low, start), (high - low, HALO), allow_negative_indices=False)

    windows = [(i * step, (i + 1) * step, 0, peak_width) for i in range(EARLY_PARTS)]
    windows += [(early, sample_rows, low, high) for low, high in groups[:-1]]
    windows += [(early, end, ends[-1], peak_width), (end, sample_rows, ends[-1], peak_width)]
    held, source = [], phenotypes
    phenotypes = near_copy(phenotypes)
    for i, (a, b, c, d) in enumerate(windows):
        piece = lax.slice(source, (a, c), (b, d))
        held.append(lax.ppermute(piece, "pos", swap))
        if i == DIRECT_CUTS - 1:
            source = phenotypes
    first, late, right, tip = held[:EARLY_PARTS], held[EARLY_PARTS:-2], held[-2], held[-1]
    passed = [lax.ppermute(x, "pos", onward) for x in first]

    far_late = lax.optimization_barrier(half_rows(far_start, early, sample_rows))
    far_in = lax.ppermute(far_late, "pos", back)

    inner_shares = list(range(halo_shares, samp_count - halo_shares))
    outer_shares = [*range(halo_shares), *range(samp_count - halo_shares, samp_count)]
    bits = [1 << i for i in range(samp_count.bit_length() - 2)]

    def pieces_of(first, second, owners):
        out = []
        for k, t in enumerate(owners):
            rows, tails = first if k < halo_shares else second
            low = (k % halo_shares) * share_rows
            piece = rows[low : low + share_rows]
            out.append((t, jnp.concatenate([piece, tails[k % halo_shares]]) if tails else piece))
        return out

    def exchange(tagged, bit):
        mine = odd_at[bit.bit_length() - 1]
        zeros = [x for x in tagged if (x[0] // bit) % 2 == 0]
        ones = [x for x in tagged if (x[0] // bit) % 2 == 1]
        kept = []
        for (tag, z), (_, o) in zip(zeros, ones):
            keep, send = jnp.where(mine, o, z), jnp.where(mine, z, o)
            kept.append((tag, keep + lax.ppermute(send, "samp", [(s, s ^ bit) for s in all_samp])))
        return kept

    parts = []
    for part in range(OWN_CALLS):
        parts.append(own_block(dosages, phenotypes, share_rows, groups[0][1], part))
    *own, tails = [sum(x[1:], x[0]) for x in zip(*parts)]
    tails = [tails[k * TAIL : (k + 1) * TAIL] for k in range(len(own))]
    own = list(zip(inner_shares, own))
    low_tails, high_tails = tails[:halo_shares], tails[-halo_shares:]
    near_tails = [parity(h, l) for h, l in zip(high_tails, low_tails)]
    far_tails = [parity(l, h) for h, l in zip(high_tails, low_tails)]
    for bit in bits:
        own = exchange(own, bit)
    ((_, own),) = own
    own_total = own + lax.ppermute(own, "samp", [(t ^ half, t) for t in inner_shares])
    peak_total = jnp.maximum(own[share_rows:, peak_width - LANES :], 0.0)
    peak_total = peak_total + lax.ppermute(peak_total, "samp", [(s, s ^ half) for s in all_samp])
    peak_total = peak_total[: peak_width // LANES].reshape(peak_width)

    near_early = cross_rows(half_rows(near_start, 0, early), jnp.concatenate(first))
    far_early = cross_rows(half_rows(far_start, 0, early - step), jnp.concatenate(passed[:-1]))
    far_early = added(far_early, cross_rows(half_rows(far_start, early - step, early), passed[-1]))

    wide = [jnp.pad(x, ((0, 0), (0, peak_width - x.shape[1]))) for x in far_tails]
    acc = pieces_of(
        (parity(0.0, far_early), [parity(0.0, x) for x in wide]),
        (parity(far_early, 0.0), [parity(x, 0.0) for x in wide]),
        outer_shares,
    )
    acc = exchange(acc, 1)
    acc_pairs = [(s, b, s, d) for s in all_samp for b, d in back if halo_shares > 1 or (s + b) % 2 == 1]
    acc = [hop(x, acc_pairs) for _, x in acc]

    straight = [(t, b, t, b ^ 1) for t in outer_shares for b in all_pos]
    across = [(t ^ half, b, t, b ^ 1) for t in outer_shares for b in all_pos]

    def reduced(pieces, low, high):
        pieces = exchange(pieces, 1)
        pieces = [(t, x + y[: x.shape[0], low:high]) for (t, x), y in zip(pieces, acc)]
        for bit in bits[1:]:
            pieces = exchange(pieces, bit)
        ((_, only),) = pieces
        return only

    totals = []
    for g, ((low, high), peaks) in enumerate(zip(groups, late)):
        near_edge = near_early[:, low:high] + cross_rows(half_rows(near_start, early, sample_rows), peaks)
        far_edge = cross_rows(far_in, peaks)
        up, down = parity(near_edge, far_edge), parity(far_edge, near_edge)
        up_tails = [parity(x, 0.0) for x in near_tails] if g == 0 else None
        down_tails = [parity(0.0, x) for x in near_tails] if g == 0 else None
        edge = reduced(pieces_of((up, up_tails), (down, down_tails), outer_shares), low, high)
        totals.append(hop(edge, straight) + hop(edge, across))

    low, high = groups[-1]
    near_edge = near_early[:, low:high] + cross_rows(half_rows(near_start, early, end), right)
    far_edge = cross_rows(far_in[: end - early], right)
    near_edge = added(near_edge, cross_rows(half_rows(near_start, end, sample_rows), tip))
    far_edge = added(far_edge, cross_rows(far_in[end - early :], tip))
    up, down = parity(near_edge, far_edge), parity(far_edge, near_edge)
    edge = reduced(pieces_of((up, None), (down, None), outer_shares), low, high)
    totals.append(hop(edge, straight) + hop(edge, across))

    shares = [
        jnp.where(outer, total, own_total[: total.shape[0], low:high]) for total, (low, high) in zip(totals, groups)
    ]
    split = groups[0][1]
    variant_share = shares[0][share_rows : share_rows + share_rows // split].reshape(share_rows)
    variant_index = first_variant + jnp.arange(share_rows, dtype=jnp.int32)[:, None]
    factor = math.sqrt(float(sample_rows * samp_count - 2))

    def scale_of(low, high):
        return jnp.sqrt((variant_share[:, None] + EPS) * (peak_total[None, low:high] + EPS))

    def statistic_of(cross_share, scale, low, high):
        lows, highs = window_low[None, low:high], window_high[None, low:high]
        inside = (variant_index >= lows) & (variant_index <= highs)
        statistic = factor * cross_share / scale
        return jnp.where(inside, statistic, jnp.zeros_like(statistic))

    head = [statistic_of(x[:share_rows], scale_of(*group), *group) for x, group in zip(shares[:-1], groups)]
    head = jnp.pad(jnp.concatenate(head, axis=1), ((0, 0), (0, peak_width - ends[-1])))
    head, scale = lax.optimization_barrier((head, scale_of(*groups[-1])))
    return lax.dynamic_update_slice(head, statistic_of(shares[-1][:share_rows], scale, *groups[-1]), (0, ends[-1]))[None]


def solution(mesh):
    placed = (P("samp", "pos"), P("samp", "pos"), P("pos"), P("pos"))
    return jax.shard_map(
        statistics_share, mesh=mesh, in_specs=placed, out_specs=P("pos", "samp", None), check_vma=False
    )
```

```python
import functools
import math

import jax
import jax.numpy as jnp
from jax import lax
from jax.experimental import pallas as pl
from jax.experimental.pallas import tpu as pltpu
from jax.sharding import PartitionSpec as P


HALO = 512
EPS = 1e-06
LANES = 128
TAIL = 8
EARLY_SHARE = 8
EARLY_PARTS = 4
END_SHARE = 2
GROUP_TILES = (2,)
OWN_CALLS = 2
DIRECT_CUTS = 2
COPY_STEPS = 4
COPY_VMEM = 8 * 1024 * 1024
OWN_STEPS = 4
OWN_VMEM = 20 * 1024 * 1024


def cross_rows(variant_panel, phenotypes):
    return lax.dot_general(
        variant_panel, phenotypes, (((0,), (0,)), ((), ())), preferred_element_type=jnp.float32
    )


def added(total, part):
    return part if total is None else lax.optimization_barrier(total) + part


def folded_squares(block):
    wide = block.astype(jnp.float32)
    return jnp.sum((wide * wide).reshape(-1, 8, wide.shape[1]), axis=0)


def copy_kernel(source, copy):
    copy[...] = source[...]


def near_copy(array):
    rows = array.shape[0] // COPY_STEPS
    block = pl.BlockSpec((rows, array.shape[1]), lambda i: (i, 0))
    return pl.pallas_call(
        copy_kernel,
        grid=(COPY_STEPS,),
        in_specs=[block],
        out_specs=block,
        out_shape=jax.ShapeDtypeStruct(array.shape, array.dtype),
        compiler_params=pltpu.CompilerParams(vmem_limit_bytes=COPY_VMEM),
    )(array)


def own_kernel(share_rows, dosages, phenotypes, *refs):
    (*pieces, tails), (cross, variant_sq, peak_sq) = refs[:-3], refs[-3:]
    split = tails.shape[1]
    last = phenotypes.shape[1] - LANES

    @pl.when(pl.program_id(0) == 0)
    def _():
        for ref in (cross, variant_sq, peak_sq):
            ref[...] = jnp.zeros_like(ref)

    cross[...] += cross_rows(dosages[...], phenotypes[...])
    variant_sq[...] += folded_squares(dosages[...])
    peak_sq[...] += folded_squares(phenotypes[...])

    @pl.when(pl.program_id(0) == pl.num_programs(0) - 1)
    def _():
        variant_sums = jnp.sum(variant_sq[...], axis=0, keepdims=True)
        peak_sums = jnp.sum(peak_sq[...], axis=0, keepdims=True)
        tails[...] = jnp.zeros_like(tails)
        for k, piece in enumerate(pieces):
            first = k * share_rows
            piece[:share_rows] = cross[first : first + share_rows]
            piece[share_rows:] = jnp.zeros((TAIL, piece.shape[1]), jnp.float32)
            for row in range(share_rows // split):
                sums = variant_sums[:, first + row * split : first + (row + 1) * split]
                piece[share_rows + row : share_rows + row + 1, :split] = sums
                tails[k * TAIL + row : k * TAIL + row + 1] = sums
            for row in range(peak_sums.shape[1] // LANES):
                sums = peak_sums[:, row * LANES : (row + 1) * LANES]
                piece[share_rows + row : share_rows + row + 1, last:] = sums


def own_block(dosages, phenotypes, share_rows, split, part):
    sample_rows, block_width = dosages.shape
    peak_width = phenotypes.shape[1]
    rows = sample_rows // OWN_STEPS
    shares = block_width // share_rows
    steps = OWN_STEPS // OWN_CALLS
    shapes = [(share_rows + TAIL, peak_width)] * shares + [(shares * TAIL, split)]
    return pl.pallas_call(
        functools.partial(own_kernel, share_rows),
        grid=(steps,),
        in_specs=[
            pl.BlockSpec((rows, block_width), lambda i: (part * steps + i, 0)),
            pl.BlockSpec((rows, peak_width), lambda i: (part * steps + i, 0)),
        ],
        out_specs=[pl.BlockSpec(shape, lambda i: (0, 0)) for shape in shapes],
        out_shape=[jax.ShapeDtypeStruct(shape, jnp.float32) for shape in shapes],
        scratch_shapes=[
            pltpu.VMEM((block_width, peak_width), jnp.float32),
            pltpu.VMEM((8, block_width), jnp.float32),
            pltpu.VMEM((8, peak_width), jnp.float32),
        ],
        compiler_params=pltpu.CompilerParams(vmem_limit_bytes=OWN_VMEM),
        name="own_block",
    )(dosages, phenotypes)


def statistics_share(dosages, phenotypes, window_low, window_high):
    sample_rows, block_width = dosages.shape
    peak_width = phenotypes.shape[1]
    span_width = block_width + 2 * HALO
    samp_count = lax.axis_size("samp")
    pos_count = lax.axis_size("pos")
    samp_index = lax.axis_index("samp")
    pos_index = lax.axis_index("pos")
    share_rows = span_width // samp_count
    halo_shares = HALO // share_rows
    half = samp_count // 2
    all_samp = range(samp_count)
    all_pos = range(pos_count)
    ends = [0]
    for tiles in GROUP_TILES:
        ends.append(ends[-1] + tiles * LANES)
    groups = list(zip(ends, [*ends[1:], peak_width]))
    early = sample_rows * EARLY_SHARE // 16
    end = sample_rows - sample_rows * END_SHARE // 16
    step = early // EARLY_PARTS

    even = (pos_index & 1) == 0
    near_start = jnp.where(even, block_width - HALO, 0)
    far_start = jnp.where(even, 0, block_width - HALO)
    outer = (samp_index < halo_shares) | (samp_index >= samp_count - halo_shares)
    odd_at = [(samp_index & (1 << i)) != 0 for i in range(samp_count.bit_length() - 2)]
    first_variant = pos_index * block_width - HALO + samp_index * share_rows
    dosages, phenotypes, even, near_start, far_start, outer, odd_at, first_variant = lax.optimization_barrier(
        (dosages, phenotypes, even, near_start, far_start, outer, odd_at, first_variant)
    )

    def hop(array, pairs):
        flat = [(a * pos_count + b, c * pos_count + d) for a, b, c, d in pairs]
        return lax.ppermute(array, ("samp", "pos"), flat)

    def parity(x, y):
        return jnp.where(even, x, y)

    swap = [(b, b ^ 1) for b in all_pos]
    onward = [(b, b + 2) for b in range(0, pos_count - 2, 2)] + [(b, b - 2) for b in range(3, pos_count, 2)]
    back = [(d, s) for s, d in onward]

    def half_rows(start, low, high):
        return lax.dynamic_slice(dosages, (low, start), (high - low, HALO), allow_negative_indices=False)

    windows = [(i * step, (i + 1) * step, 0, peak_width) for i in range(EARLY_PARTS)]
    windows += [(early, sample_rows, low, high) for low, high in groups[:-1]]
    windows += [(early, end, ends[-1], peak_width), (end, sample_rows, ends[-1], peak_width)]
    held, source = [], phenotypes
    phenotypes = near_copy(phenotypes)
    for i, (a, b, c, d) in enumerate(windows):
        piece = lax.slice(source, (a, c), (b, d))
        held.append(lax.ppermute(piece, "pos", swap))
        if i == DIRECT_CUTS - 1:
            source = phenotypes
    first, late, right, tip = held[:EARLY_PARTS], held[EARLY_PARTS:-2], held[-2], held[-1]
    passed = [lax.ppermute(x, "pos", onward) for x in first]

    far_late = lax.optimization_barrier(half_rows(far_start, early, sample_rows))
    far_in = lax.ppermute(far_late, "pos", back)

    inner_shares = list(range(halo_shares, samp_count - halo_shares))
    outer_shares = [*range(halo_shares), *range(samp_count - halo_shares, samp_count)]
    bits = [1 << i for i in range(samp_count.bit_length() - 2)]

    def pieces_of(first, second, owners):
        out = []
        for k, t in enumerate(owners):
            rows, tails = first if k < halo_shares else second
            low = (k % halo_shares) * share_rows
            piece = rows[low : low + share_rows]
            out.append((t, jnp.concatenate([piece, tails[k % halo_shares]]) if tails else piece))
        return out

    def exchange(tagged, bit):
        mine = odd_at[bit.bit_length() - 1]
        zeros = [x for x in tagged if (x[0] // bit) % 2 == 0]
        ones = [x for x in tagged if (x[0] // bit) % 2 == 1]
        kept = []
        for (tag, z), (_, o) in zip(zeros, ones):
            keep, send = jnp.where(mine, o, z), jnp.where(mine, z, o)
            kept.append((tag, keep + lax.ppermute(send, "samp", [(s, s ^ bit) for s in all_samp])))
        return kept

    parts = []
    for part in range(OWN_CALLS):
        parts.append(own_block(dosages, phenotypes, share_rows, groups[0][1], part))
    *own, tails = [sum(x[1:], x[0]) for x in zip(*parts)]
    tails = [tails[k * TAIL : (k + 1) * TAIL] for k in range(len(own))]
    own = list(zip(inner_shares, own))
    low_tails, high_tails = tails[:halo_shares], tails[-halo_shares:]
    near_tails = [parity(h, l) for h, l in zip(high_tails, low_tails)]
    far_tails = [parity(l, h) for h, l in zip(high_tails, low_tails)]
    for bit in bits:
        own = exchange(own, bit)
    ((_, own),) = own
    own_total = own + lax.ppermute(own, "samp", [(t ^ half, t) for t in inner_shares])
    peak_total = jnp.maximum(own[share_rows:, peak_width - LANES :], 0.0)
    peak_total = peak_total + lax.ppermute(peak_total, "samp", [(s, s ^ half) for s in all_samp])
    peak_total = peak_total[: peak_width // LANES].reshape(peak_width)

    near_early = cross_rows(half_rows(near_start, 0, early), jnp.concatenate(first))
    far_early = cross_rows(half_rows(far_start, 0, early - step), jnp.concatenate(passed[:-1]))
    far_early = added(far_early, cross_rows(half_rows(far_start, early - step, early), passed[-1]))

    wide = [jnp.pad(x, ((0, 0), (0, peak_width - x.shape[1]))) for x in far_tails]
    acc = pieces_of(
        (parity(0.0, far_early), [parity(0.0, x) for x in wide]),
        (parity(far_early, 0.0), [parity(x, 0.0) for x in wide]),
        outer_shares,
    )
    acc = exchange(acc, 1)
    acc_pairs = [(s, b, s, d) for s in all_samp for b, d in back if halo_shares > 1 or (s + b) % 2 == 1]
    acc = [hop(x, acc_pairs) for _, x in acc]

    straight = [(t, b, t, b ^ 1) for t in outer_shares for b in all_pos]
    across = [(t ^ half, b, t, b ^ 1) for t in outer_shares for b in all_pos]

    def reduced(pieces, low, high):
        pieces = exchange(pieces, 1)
        pieces = [(t, x + y[: x.shape[0], low:high]) for (t, x), y in zip(pieces, acc)]
        for bit in bits[1:]:
            pieces = exchange(pieces, bit)
        ((_, only),) = pieces
        return only

    totals = []
    for g, ((low, high), peaks) in enumerate(zip(groups, late)):
        near_edge = near_early[:, low:high] + cross_rows(half_rows(near_start, early, sample_rows), peaks)
        far_edge = cross_rows(far_in, peaks)
        up, down = parity(near_edge, far_edge), parity(far_edge, near_edge)
        up_tails = [parity(x, 0.0) for x in near_tails] if g == 0 else None
        down_tails = [parity(0.0, x) for x in near_tails] if g == 0 else None
        edge = reduced(pieces_of((up, up_tails), (down, down_tails), outer_shares), low, high)
        totals.append(hop(edge, straight) + hop(edge, across))

    low, high = groups[-1]
    near_edge = near_early[:, low:high] + cross_rows(half_rows(near_start, early, end), right)
    far_edge = cross_rows(far_in[: end - early], right)
    near_edge = added(near_edge, cross_rows(half_rows(near_start, end, sample_rows), tip))
    far_edge = added(far_edge, cross_rows(far_in[end - early :], tip))
    up, down = parity(near_edge, far_edge), parity(far_edge, near_edge)
    edge = reduced(pieces_of((up, None), (down, None), outer_shares), low, high)
    totals.append(hop(edge, straight) + hop(edge, across))

    shares = [
        jnp.where(outer, total, own_total[: total.shape[0], low:high]) for total, (low, high) in zip(totals, groups)
    ]
    split = groups[0][1]
    variant_share = shares[0][share_rows : share_rows + share_rows // split].reshape(share_rows)
    variant_index = first_variant + jnp.arange(share_rows, dtype=jnp.int32)[:, None]
    factor = math.sqrt(float(sample_rows * samp_count - 2))

    def statistic_of(cross_share, low, high):
        lows, highs = window_low[None, low:high], window_high[None, low:high]
        inside = (variant_index >= lows) & (variant_index <= highs)
        scale_terms = (variant_share[:, None] + EPS) * (peak_total[None, low:high] + EPS)
        statistic = factor * cross_share / jnp.sqrt(scale_terms)
        return jnp.where(inside, statistic, jnp.zeros_like(statistic))

    head = [statistic_of(x[:share_rows], *group) for x, group in zip(shares[:-1], groups)]
    head = jnp.pad(jnp.concatenate(head, axis=1), ((0, 0), (0, peak_width - ends[-1])))
    head = lax.optimization_barrier(head)
    return lax.dynamic_update_slice(head, statistic_of(shares[-1][:share_rows], *groups[-1]), (0, ends[-1]))[None]


def solution(mesh):
    placed = (P("samp", "pos"), P("samp", "pos"), P("pos"), P("pos"))
    return jax.shard_map(
        statistics_share, mesh=mesh, in_specs=placed, out_specs=P("pos", "samp", None), check_vma=False
    )
```
